32 devices in a mesh: series: 4 (over y, x), tm: 8 (over z, core).
Axes of the slice: x: 2, y: 2, z: 4, core: 2. Of those that a mesh axis runs over, the one named last changes fastest.
Arguments:
- observed: bfloat16 [8192, 8192], P('series', 'tm'), may hold values from -6 to 6
- mask: bfloat16 [8192, 8192], P('series', 'tm'), may hold values from 0 to 1, as said below
- loadings: float32 [8192, 128], P('series'), may hold values from -0.5 to 0.5
- factors: float32 [8192, 128], P('tm'), may hold values from -6 to 6
- lag_weights: float32 [2, 128], replicated, may hold values from 0.2 to 0.7
Outputs:
- new_loadings: float32 [8192, 128], P('series')
- new_factors: float32 [8192, 128], P('tm')
The draws below stay inside these ranges and needn't reach their ends.
Inputs may be any that keep to these rules, and one draw needn't show every extreme that they name: `mask`: each entry is 0 or 1.
All inputs are finite; a program needn't handle non-finite values.
Results may differ from the reference program's by a relative error of at most 0.0041.
Values sent between devices are 32-bit elements; how exact they have to be, the bound alone decides.
No kernel may reach another device: no remote copies, remote signals or barrier semaphores. Data moves between devices by JAX's collectives and lax.ppermute only.
A program may use at most 128 MiB of HBM per device.

```python
import jax
import jax.numpy as jnp
from jax import lax

RANK = 128
LAG = 1440
OUTER = 2
TIME_STEPS = 2
SERIES = 8192
MINUTES = 8192


def draw_mask(key, part):
    sample = jax.random.uniform(jax.random.fold_in(key, 17), (SERIES, MINUTES), jnp.float32)
    return jnp.where(sample < 0.7, 1.0, 0.0).astype(jnp.float32).astype(jnp.bfloat16)


def block_scale(rng, extent, pieces, low, top_value):
    level, own = 1.0, jax.random.fold_in(rng, 6)
    for axis_at, shards_of in pieces:
        draws = jnp.exp(jax.random.uniform(jax.random.fold_in(own, axis_at), (shards_of,), jnp.float32, low / len(pieces), top_value / len(pieces)))
        level = level * jnp.repeat(draws, extent[axis_at] // shards_of).reshape([-1 if axis == axis_at else 1 for axis in range(len(extent))])
    return level


def bell_draw(own_key, shape, spread, reach, pieces=(), held_as=jnp.bfloat16):
    drawn = jax.random.normal(own_key, shape, jnp.float32) * spread
    if len(pieces) > 0:
        drawn = block_scale(own_key, shape, pieces, -0.22, 0.18) * drawn
    return jnp.clip(drawn, min=-reach, max=reach).astype(held_as)


def setup_inputs(seed: int = 0) -> dict:
    splits = jax.random.split(jax.random.key(seed), 6)
    return {
        "observed": bell_draw(splits[0], (SERIES, MINUTES), 1.0, 6.0, ((0, 4), (1, 8))),
        "mask": draw_mask(jax.random.fold_in(splits[5], 71), 0),
        "loadings": bell_draw(splits[2], (SERIES, RANK), RANK ** -0.5, 0.5, ((0, 4),), jnp.float32),
        "factors": bell_draw(splits[3], (MINUTES, RANK), 1.0, 6.0, ((0, 8),), jnp.float32),
        "lag_weights": jnp.clip(jax.random.uniform(splits[4], (2, RANK), jnp.float32, 0.2, 0.7), 0.2, 0.7),
    }


smooth = 4.0
shrink = 0.1
margin = 32.0

def back(z, lag):
    return jnp.concatenate([jnp.zeros((lag, z.shape[1]), jnp.float32), z[:-lag]], axis=0)

def ahead(z, lag):
    return jnp.concatenate([z[lag:], jnp.zeros((lag, z.shape[1]), jnp.float32)], axis=0)

def block_residual(observed, mask, fb, xb):
    prod = lax.dot_general(fb, xb, (((1,), (1,)), ((), ())), preferred_element_type=jnp.float32)
    return (mask.astype(jnp.float32) * (prod - observed.astype(jnp.float32))).astype(jnp.bfloat16)

def reference(observed, mask, loadings, factors, lag_weights):
    step_time = 1.0 / (SERIES / RANK + margin)
    step_load = 1.0 / MINUTES
    block = min(2048, SERIES)
    count = SERIES // block
    obs_blocks = observed.reshape(count, block, MINUTES)
    mask_blocks = mask.reshape(count, block, MINUTES)
    loads = loadings
    times = factors
    for outer in range(OUTER):
        for inner in range(TIME_STEPS):
            fb = loads.astype(jnp.bfloat16).reshape(count, block, RANK)
            xb = times.astype(jnp.bfloat16)

            def accumulate(total, items):
                obs_b, mask_b, fb_b = items
                rb = block_residual(obs_b, mask_b, fb_b, xb)
                return (total + lax.dot_general(rb, fb_b, (((0,), (0,)), ((), ())), preferred_element_type=jnp.float32), None)
            grad, unused = lax.scan(accumulate, jnp.zeros((MINUTES, RANK), jnp.float32), (obs_blocks, mask_blocks, fb))
            resid = times - lag_weights[0] * back(times, 1) - lag_weights[1] * back(times, LAG)
            smooth_grad = smooth * (resid - lag_weights[0] * ahead(resid, 1) - lag_weights[1] * ahead(resid, LAG))
            times = times - step_time * (grad + smooth_grad)
        fb = loads.astype(jnp.bfloat16).reshape(count, block, RANK)
        xb = times.astype(jnp.bfloat16)

        def loading_grad(items):
            obs_b, mask_b, fb_b = items
            rb = block_residual(obs_b, mask_b, fb_b, xb)
            return jnp.dot(rb, xb, preferred_element_type=jnp.float32)
        grad_f = lax.map(loading_grad, (obs_blocks, mask_blocks, fb)).reshape(SERIES, RANK)
        loads = loads - step_load * (grad_f + shrink * loads)
    return (loads, times)
```

```python
import jax
import jax.numpy as jnp
from jax import lax
from jax.experimental import pallas as pl
from jax.experimental.pallas import tpu as pltpu
from jax.sharding import PartitionSpec as P

LAG = 1440
OUTER = 2
TIME_STEPS = 2

smooth = 4.0
shrink = 0.1
margin = 32.0
hidden = 64.0
PAD = 8
F32 = jnp.float32
BF16 = jnp.bfloat16
VMEM = pl.BlockSpec(memory_space=pltpu.VMEM)
ANY = pl.BlockSpec(memory_space=pl.ANY)


def dot_nt(a, b):
    return lax.dot_general(a, b, (((1,), (1,)), ((), ())), preferred_element_type=F32)


def dot_tn(a, b):
    return lax.dot_general(a, b, (((0,), (0,)), ((), ())), preferred_element_type=F32)


def dot_nn(a, b):
    return lax.dot_general(a, b, (((1,), (0,)), ((), ())), preferred_element_type=F32)


def up8(value):
    return -(-value // 8) * 8


class Plan:
    def __init__(self, n_s, n_t, series, minutes, rank):
        self.n_s, self.n_t, self.series, self.minutes, self.rank = n_s, n_t, series, minutes, rank
        self.rows = minutes // n_s
        self.n_z = n_t // 2
        self.block = series // n_t
        self.half = series // 2
        need = []
        for s in range(n_s):
            first = s * self.rows
            by_delta = {}
            spans = [("back", first - LAG, self.rows + 1), ("far", first + LAG - 1, self.rows + 1)]
            if s == 0:
                spans.append(("prev", -1, 1))
            if s == n_s - 1:
                spans.append(("next", minutes, 1))
            for kind, row, count in spans:
                at = 0
                while at < count:
                    delta = (row + at) // minutes
                    local = (row + at) % minutes
                    size = min(count - at, minutes - local)
                    assert delta != 0
                    by_delta.setdefault(delta, []).append((kind, at, local, size))
                    at += size
            order = sorted(by_delta.items(), key=lambda item: (-sum(p[3] for p in item[1]), item[0]))
            need.append(order)
        self.slots = max(len(order) for order in need)
        self.pieces = []
        self.length = []
        self.pairs = []
        for slot in range(self.slots):
            per_s, pairs, length = [], [], 8
            for s in range(n_s):
                placed, offset = [], 0
                if slot < len(need[s]):
                    delta, parts = need[s][slot]
                    for kind, at, local, size in parts:
                        placed.append((kind, at, local, size, offset))
                        offset += up8(size)
                    for t in range(n_t):
                        if 0 <= t + delta < n_t:
                            pairs.append((s * n_t + t + delta, s * n_t + t))
                length = max(length, offset)
                per_s.append(placed)
            self.pieces.append(per_s)
            self.length.append(length)
            self.pairs.append(pairs)


def load_x(plan, x_refs, xs):
    s = lax.axis_index("series")
    rows = plan.rows
    if len(x_refs) == 1:
        xs[pl.ds(PAD, plan.minutes), :] = x_refs[0][...]
    else:
        for k in range(plan.n_s):
            start = pl.multiple_of(PAD + jnp.bitwise_xor(s, k) * rows, 8)
            xs[pl.ds(start, rows), :] = x_refs[k][...]


def pack_halo(plan, xs, h_refs, win):
    s = lax.axis_index("series")
    start = pl.multiple_of(s * plan.rows, 8)
    win[...] = xs[pl.ds(start, plan.rows + 2 * PAD), :]
    for value in range(plan.n_s):
        @pl.when(s == value)
        def _():
            for slot in range(plan.slots):
                for kind, at, local, size, offset in plan.pieces[slot][value]:
                    h_refs[slot][pl.ds(offset, size), :] = xs[pl.ds(PAD + local, size), :]


def residual(prod, obs):
    obs = obs.astype(F32)
    return jnp.where(obs < 0.5 * hidden, prod - obs, 0.0).astype(BF16)


def halo_shapes(plan):
    shapes = [jax.ShapeDtypeStruct((length, plan.rank), F32) for length in plan.length]
    return shapes + [jax.ShapeDtypeStruct((plan.rows + 2 * PAD, plan.rank), F32)]


def time_pass(plan, data, loads, xp, halo):
    first = len(data) == 2
    n_s, rows, series, minutes, rank = plan.n_s, plan.rows, plan.series, plan.minutes, plan.rank
    chunk = series // 4
    count = series // chunk
    n_x = len(xp)
    n_h = plan.slots + 1 if halo else 0

    def kernel(*refs):
        refs = list(refs)
        d_refs = [refs.pop(0) for _ in data]
        f = refs.pop(0)
        x_refs = [refs.pop(0) for _ in range(n_x)]
        g_refs = [refs.pop(0) for _ in range(n_s)]
        h_refs = [refs.pop(0) for _ in range(n_h)]
        packed = refs.pop(0) if first else None
        bufs = [refs.pop(0) for _ in data]
        xs, acc, sem = refs
        copies = []
        for c in range(count):
            span = pl.ds(c * chunk, chunk)
            copies.append([pltpu.make_async_copy(d.at[span, :], b.at[span, :], sem.at[i, c])
                           for i, (d, b) in enumerate(zip(d_refs, bufs))])
        for group in copies:
            for copy in group:
                copy.start()
        load_x(plan, x_refs, xs)
        if halo:
            pack_halo(plan, xs, h_refs[:-1], h_refs[-1])
        xb = xs[pl.ds(PAD, minutes), :].astype(BF16)
        outs = []
        for c in range(count):
            span = pl.ds(c * chunk, chunk)
            for copy in copies[c]:
                copy.wait()
            if first:
                kept = jnp.where(bufs[1][span, :] > 0, bufs[0][span, :], jnp.full((), hidden, BF16))
                bufs[0][span, :] = kept
                out = pltpu.make_async_copy(bufs[0].at[span, :], packed.at[span, :], sem.at[2, c])
                out.start()
                outs.append(out)
            fb = f[span, :].astype(BF16)
            part = dot_tn(fb, residual(dot_nt(fb, xb), bufs[0][span, :]))
            if c == 0:
                acc[...] = part
            else:
                acc[...] += part
        s = lax.axis_index("series")
        for k in range(n_s):
            start = pl.multiple_of(jnp.bitwise_xor(s, k) * rows, 128)
            g_refs[k][...] = acc[:, pl.ds(start, rows)].T
        for out in outs:
            out.wait()

    out_shape = [jax.ShapeDtypeStruct((rows, rank), F32) for _ in range(n_s)]
    out_specs = [VMEM] * n_s
    if halo:
        out_shape += halo_shapes(plan)
        out_specs += [VMEM] * n_h
    if first:
        out_shape.append(jax.ShapeDtypeStruct((series, minutes), BF16))
        out_specs.append(ANY)
    outs = pl.pallas_call(
        kernel,
        in_specs=[ANY] * len(data) + [VMEM] * (1 + n_x),
        out_specs=out_specs,
        out_shape=out_shape,
        scratch_shapes=[pltpu.VMEM((series, minutes), BF16) for _ in data]
        + [pltpu.VMEM((minutes + 2 * PAD, rank), F32), pltpu.VMEM((rank, minutes), F32),
           pltpu.SemaphoreType.DMA((3, count))],
        name="time_pass",
    )(*data, loads, *xp)
    outs = list(outs)
    grads = outs[:n_s]
    halos = outs[n_s:n_s + n_h]
    return grads, halos, (outs[-1] if first else None)


def load_pass(plan, data, loads, xp, halo):
    n_s, series, minutes, rank = plan.n_s, plan.series, plan.minutes, plan.rank
    block, n_z, half = plan.block, plan.n_z, plan.half
    n_x = len(xp)
    n_h = plan.slots + 1 if halo else 1
    count = 2 * n_z

    def kernel(*refs):
        refs = list(refs)
        d = refs.pop(0)
        f = refs.pop(0)
        x_refs = [refs.pop(0) for _ in range(n_x)]
        other = refs.pop(0)
        mine = [refs.pop(0) for _ in range(n_z)]
        h_refs = [refs.pop(0) for _ in range(n_h)]
        buf, xs, sem = refs
        t = lax.axis_index("tm")
        core, z = t % 2, t // 2
        spans, copies = [], []
        for c in range(count):
            side = core if c >= n_z else 1 - core
            start = pl.multiple_of(side * half + jnp.bitwise_xor(z, c % n_z) * block, block)
            spans.append(pl.ds(start, block))
            copies.append(pltpu.make_async_copy(d.at[spans[c], :], buf.at[pl.ds(c * block, block), :], sem.at[c]))
        for copy in copies:
            copy.start()
        load_x(plan, x_refs, xs)
        xb = xs[pl.ds(PAD, minutes), :].astype(BF16)
        for c in range(count):
            copies[c].wait()
            fb = f[spans[c], :].astype(BF16)
            rb = residual(dot_nt(fb, xb), buf[pl.ds(c * block, block), :])
            part = dot_nn(rb, xb)
            if c < n_z:
                other[pl.ds(c * block, block), :] = part
            else:
                mine[c - n_z][...] = part
        if halo:
            pack_halo(plan, xs, h_refs[:-1], h_refs[-1])
        else:
            h_refs[0][...] = xs[pl.ds(PAD, minutes), :]

    out_shape = [jax.ShapeDtypeStruct((half, rank), F32)]
    out_shape += [jax.ShapeDtypeStruct((block, rank), F32) for _ in range(n_z)]
    out_shape += halo_shapes(plan) if halo else [jax.ShapeDtypeStruct((minutes, rank), F32)]
    outs = pl.pallas_call(
        kernel,
        in_specs=[ANY] + [VMEM] * (1 + n_x),
        out_specs=[VMEM] * len(out_shape),
        out_shape=out_shape,
        scratch_shapes=[pltpu.VMEM((series, minutes), BF16), pltpu.VMEM((minutes + 2 * PAD, rank), F32),
                        pltpu.SemaphoreType.DMA((count,))],
        name="load_pass",
    )(data, loads, *xp)
    outs = list(outs)
    return outs[0], outs[1:1 + n_z], outs[1 + n_z:]


def smoothing(plan, win, halos, lag_weights):
    rows, rank = plan.rows, plan.rank
    total = plan.minutes * plan.n_t

    def kernel(*refs):
        refs = list(refs)
        win_ref = refs.pop(0)
        h_refs = [refs.pop(0) for _ in range(plan.slots)]
        w_ref, out, xw, far, near = refs
        s = lax.axis_index("series")
        t = lax.axis_index("tm")
        xw[...] = win_ref[...]
        for value in range(plan.n_s):
            @pl.when(s == value)
            def _():
                for slot in range(plan.slots):
                    for kind, at, local, size, offset in plan.pieces[slot][value]:
                        target, place = {"back": (near, at), "far": (far, at),
                                         "prev": (xw, PAD - 1), "next": (xw, PAD + rows)}[kind]
                        target[pl.ds(place, size), :] = h_refs[slot][pl.ds(offset, size), :]
        w0 = w_ref[0:1, :]
        w1 = w_ref[1:2, :]
        x = xw[pl.ds(PAD, rows), :]
        here = t * plan.minutes + s * rows + lax.broadcasted_iota(jnp.int32, (rows, rank), 0)
        resid = x - w0 * xw[pl.ds(PAD - 1, rows), :] - w1 * near[pl.ds(0, rows), :]
        after_one = xw[pl.ds(PAD + 1, rows), :] - w0 * x - w1 * near[pl.ds(1, rows), :]
        after_far = far[pl.ds(1, rows), :] - w0 * far[pl.ds(0, rows), :] - w1 * x
        after_one = jnp.where(here + 1 < total, after_one, 0.0)
        after_far = jnp.where(here + LAG < total, after_far, 0.0)
        out[...] = smooth * (resid - w0 * after_one - w1 * after_far)

    return pl.pallas_call(
        kernel,
        in_specs=[VMEM] * (2 + plan.slots),
        out_specs=VMEM,
        out_shape=jax.ShapeDtypeStruct((rows, rank), F32),
        scratch_shapes=[pltpu.VMEM((rows + 2 * PAD, rank), F32), pltpu.VMEM((up8(rows + 1), rank), F32),
                        pltpu.VMEM((up8(rows + 1), rank), F32)],
        name="smoothing",
    )(win, *halos, lag_weights)


def assemble(plan, mine, other):
    def kernel(*refs):
        blocks, (full, low) = refs[:2 * plan.n_z], refs[2 * plan.n_z:]
        t = lax.axis_index("tm")
        core, z = t % 2, t // 2
        for c in range(2 * plan.n_z):
            side = core if c < plan.n_z else 1 - core
            start = side * plan.half + jnp.bitwise_xor(z, c % plan.n_z) * plan.block
            span = pl.ds(pl.multiple_of(start, plan.block), plan.block)
            value = blocks[c][...]
            full[span, :] = value
            low[span, :] = value.astype(BF16)

    shape = (plan.series, plan.rank)
    return pl.pallas_call(
        kernel,
        in_specs=[VMEM] * (2 * plan.n_z),
        out_specs=[VMEM, VMEM],
        out_shape=[jax.ShapeDtypeStruct(shape, F32), jax.ShapeDtypeStruct(shape, BF16)],
        name="assemble",
    )(*mine, *other)


def body(observed, mask, loadings, factors, lag_weights):
    n_s, n_t = lax.axis_size("series"), lax.axis_size("tm")
    plan = Plan(n_s, n_t, loadings.shape[0], factors.shape[0], loadings.shape[1])
    step_time = 1.0 / (plan.series * n_s / plan.rank + margin)
    step_load = 1.0 / (plan.minutes * n_t)
    rows, n_z, block = plan.rows, plan.n_z, plan.block

    def swap(value, axis, count, k):
        return lax.ppermute(value, axis, [(i, i ^ k) for i in range(count)])

    t = lax.axis_index("tm")
    own_start = (t % 2) * plan.half + (t // 2) * block
    own_loads = lax.dynamic_slice_in_dim(loadings, own_start, block, 0)
    loads = loadings
    data = (observed, mask)
    xp = [factors]
    halos = None
    for outer in range(OUTER):
        for inner in range(TIME_STEPS):
            grads, made, packed = time_pass(plan, data, loads, xp, halos is None)
            if packed is not None:
                data = (packed,)
            if halos is None:
                halos = made
            got = [swap(grads[k], "series", n_s, k) for k in range(1, n_s)]
            sent = [lax.ppermute(h, ("series", "tm"), pairs) for h, pairs in zip(halos[:-1], plan.pairs)]
            win = halos[-1]
            smooth_grad = smoothing(plan, win, sent, lag_weights)
            share = grads[0]
            for value in got:
                share = share + value
            own = win[PAD:PAD + rows] - step_time * (share + smooth_grad)
            xp = [own] + [swap(own, "series", n_s, k) for k in range(1, n_s)]
            halos = None
        other, mine, made = load_pass(plan, data[0], loads, xp, outer + 1 < OUTER)
        halos = made
        crossed = swap(other, "tm", n_t, 1)
        mine = [m + crossed[k * block:(k + 1) * block] for k, m in enumerate(mine)]
        total = mine[0]
        for k in range(1, n_z):
            total = total + swap(mine[k], "tm", n_t, 2 * k)
        own_loads = own_loads - step_load * (total + shrink * own_loads)
        near = [own_loads] + [swap(own_loads, "tm", n_t, 2 * k) for k in range(1, n_z)]
        far = [swap(value, "tm", n_t, 1) for value in near]
        full, loads = assemble(plan, near, far)
    return (full, made[0])


def solution(mesh):
    in_specs = (P("series", "tm"), P("series", "tm"), P("series", None), P("tm", None), P())
    out_specs = (P("series", None), P("tm", None))
    return jax.shard_map(body, mesh=mesh, in_specs=in_specs, out_specs=out_specs, check_vma=False)
```

```python
import jax
import jax.numpy as jnp
from jax import lax
from jax.experimental import pallas as pl
from jax.experimental.pallas import tpu as pltpu
from jax.sharding import PartitionSpec as P

LAG = 1440
OUTER = 2
TIME_STEPS = 2

smooth = 4.0
shrink = 0.1
margin = 32.0
hidden = 64.0
PAD = 8
F32 = jnp.float32
BF16 = jnp.bfloat16
VMEM = pl.BlockSpec(memory_space=pltpu.VMEM)
HBM = pl.BlockSpec(memory_space=pltpu.HBM)


def dot_nt(a, b):
    return lax.dot_general(a, b, (((1,), (1,)), ((), ())), preferred_element_type=F32)


def dot_tn(a, b):
    return lax.dot_general(a, b, (((0,), (0,)), ((), ())), preferred_element_type=F32)


def dot_nn(a, b):
    return lax.dot_general(a, b, (((1,), (0,)), ((), ())), preferred_element_type=F32)


def grant(mib):
    return pltpu.CompilerParams(vmem_limit_bytes=mib * 2**20)


def up8(value):
    return -(-value // 8) * 8


class Plan:
    def __init__(self, n_s, n_t, series, minutes, rank):
        self.n_s, self.n_t, self.series, self.minutes, self.rank = n_s, n_t, series, minutes, rank
        self.rows = minutes // n_s
        self.n_z = n_t // 2
        self.block = series // n_t
        self.half = series // 2
        self.need = []
        for s in range(n_s):
            first = s * self.rows
            spans = [("back", first - LAG, self.rows + 1), ("far", first + LAG - 1, self.rows + 1)]
            if s == 0:
                spans.append(("prev", -1, 1))
            if s == n_s - 1:
                spans.append(("next", minutes, 1))
            by_delta, filled = {}, {}
            for kind, row, count in spans:
                at = 0
                while at < count:
                    delta = (row + at) // minutes
                    local = (row + at) % minutes
                    size = min(count - at, minutes - local)
                    assert delta != 0
                    offset = filled.get(delta, 0)
                    by_delta.setdefault(delta, []).append((kind, at, local, size, offset))
                    filled[delta] = offset + up8(size)
                    at += size
            self.need.append((by_delta, filled))
        reach = max(abs(delta) for by_delta, filled in self.need for delta in by_delta)
        self.exchanges = [(step, parity) for step in range(1, reach + 1) for parity in (0, 1)]
        self.length, self.pairs = [], []
        for step, parity in self.exchanges:
            sizes = [filled.get(delta, 0) for by_delta, filled in self.need for delta in (step, -step)]
            self.length.append(max(sizes + [8]))
            self.pairs.append([(t, t + self.delta(e, t)) for e in [(step, parity)] for t in range(n_t)
                               if 0 <= t + self.delta(e, t) < n_t])

    def delta(self, exchange, t):
        step, parity = exchange
        return step if (t // step) % 2 == parity else -step

    def each_part(self, sending, act):
        s = lax.axis_index("series")
        t = lax.axis_index("tm")
        for value in range(self.n_s):
            for step in sorted({step for step, parity in self.exchanges}):
                for low in (0, 1):
                    slots = [(slot, e) for slot, e in enumerate(self.exchanges) if e[0] == step]

                    @pl.when(jnp.logical_and(s == value, (t // step) % 2 == low))
                    def _():
                        for slot, exchange in slots:
                            delta = self.delta(exchange, low * step)
                            for part in self.need[value][0].get(-delta if sending else delta, []):
                                act(slot, part)


def load_x(plan, x_refs, xs):
    s = lax.axis_index("series")
    rows = plan.rows
    if len(x_refs) == 1:
        xs[pl.ds(PAD, plan.minutes), :] = x_refs[0][...]
    else:
        for k in range(plan.n_s):
            start = pl.multiple_of(PAD + jnp.bitwise_xor(s, k) * rows, 8)
            xs[pl.ds(start, rows), :] = x_refs[k][...]


def pack_halo(plan, xs, h_refs, win):
    s = lax.axis_index("series")
    start = pl.multiple_of(s * plan.rows, 8)
    win[...] = xs[pl.ds(start, plan.rows + 2 * PAD), :]

    def act(slot, part):
        kind, at, local, size, offset = part
        h_refs[slot][pl.ds(offset, size), :] = xs[pl.ds(PAD + local, size), :]

    plan.each_part(True, act)


def residual(prod, obs):
    obs = obs.astype(F32)
    return jnp.where(obs < 0.5 * hidden, prod - obs, 0.0).astype(BF16)


def halo_shapes(plan):
    shapes = [jax.ShapeDtypeStruct((length, plan.rank), F32) for length in plan.length]
    return shapes + [jax.ShapeDtypeStruct((plan.rows + 2 * PAD, plan.rank), F32)]


def block_start(plan, c):
    t = lax.axis_index("tm")
    core, z = t % 2, t // 2
    side = core if c < plan.n_z else 1 - core
    return pl.multiple_of(side * plan.half + jnp.bitwise_xor(z, c % plan.n_z) * plan.block, plan.block)


def time_pass(plan, data, loads, xp, halo):
    first = len(data) == 2
    n_s, rows, series, minutes, rank = plan.n_s, plan.rows, plan.series, plan.minutes, plan.rank
    chunk = series // 4
    count = series // chunk
    n_x, n_f = len(xp), len(loads)
    n_h = len(plan.exchanges) + 1 if halo else 0

    def kernel(*refs):
        refs = list(refs)
        d_refs = [refs.pop(0) for _ in data]
        f_refs = [refs.pop(0) for _ in loads]
        x_refs = [refs.pop(0) for _ in range(n_x)]
        g_refs = [refs.pop(0) for _ in range(n_s)]
        h_refs = [refs.pop(0) for _ in range(n_h)]
        f = f_refs[0]
        if n_f > 1:
            f = refs.pop(0)
        held = refs.pop(0) if first else d_refs[0]
        xs, acc = refs[:2]
        if first:
            seen, sem = refs[2:]
            copies = []
            for c in range(count):
                span = pl.ds(c * chunk, chunk)
                copies.append([pltpu.make_async_copy(src.at[span, :], dst.at[span, :], sem.at[i, c])
                               for i, (src, dst) in enumerate(zip(d_refs, (held, seen)))])
            for group in copies:
                for copy in group:
                    copy.start()
        load_x(plan, x_refs, xs)
        if n_f > 1:
            for c in range(n_f):
                f[pl.ds(block_start(plan, c), plan.block), :] = f_refs[c][...].astype(BF16)
        if halo:
            pack_halo(plan, xs, h_refs[:-1], h_refs[-1])
        xb = xs[pl.ds(PAD, minutes), :].astype(BF16)
        for c in range(count):
            span = pl.ds(c * chunk, chunk)
            if first:
                for copy in copies[c]:
                    copy.wait()
                held[span, :] = jnp.where(seen[span, :] > 0, held[span, :], jnp.full((), hidden, BF16))
            fb = f[span, :].astype(BF16)
            part = dot_tn(fb, residual(dot_nt(fb, xb), held[span, :]))
            if c == 0:
                acc[...] = part
            else:
                acc[...] += part
        s = lax.axis_index("series")
        for k in range(n_s):
            start = pl.multiple_of(jnp.bitwise_xor(s, k) * rows, 128)
            g_refs[k][...] = acc[:, pl.ds(start, rows)].T

    out_shape = [jax.ShapeDtypeStruct((rows, rank), F32) for _ in range(n_s)]
    if halo:
        out_shape += halo_shapes(plan)
    if n_f > 1:
        out_shape.append(jax.ShapeDtypeStruct((series, rank), BF16))
    if first:
        out_shape.append(jax.ShapeDtypeStruct((series, minutes), BF16))
    scratch = [pltpu.VMEM((minutes + 2 * PAD, rank), F32), pltpu.VMEM((rank, minutes), F32)]
    if first:
        scratch += [pltpu.VMEM((series, minutes), BF16), pltpu.SemaphoreType.DMA((2, count))]
    outs = list(pl.pallas_call(
        kernel,
        in_specs=[HBM if first else VMEM] * len(data) + [VMEM] * (n_f + n_x),
        out_specs=[VMEM] * len(out_shape),
        out_shape=out_shape,
        scratch_shapes=scratch,
        compiler_params=grant(54 if first else 16),
        name="time_pass",
    )(*data, *loads, *xp))
    grads = outs[:n_s]
    halos = outs[n_s:n_s + n_h]
    return grads, halos, outs[n_s + n_h:]


def load_pass(plan, data, f, xp, other, halo, whole):
    series, minutes, rank = plan.series, plan.minutes, plan.rank
    block, n_z = plan.block, plan.n_z
    n_x = len(xp)
    n_h = len(plan.exchanges) + 1 if halo else 0

    def kernel(*refs):
        refs = list(refs)
        d, f_ref = refs.pop(0), refs.pop(0)
        x_refs = [refs.pop(0) for _ in range(n_x)]
        g_refs = [refs.pop(0) for _ in range(1 if other else n_z)]
        h_refs = [refs.pop(0) for _ in range(n_h)]
        x_out = refs.pop(0) if whole else None
        xs = refs[0]
        load_x(plan, x_refs, xs)
        xb = xs[pl.ds(PAD, minutes), :].astype(BF16)
        for c in range(n_z):
            span = pl.ds(block_start(plan, c + n_z if other else c), block)
            rb = residual(dot_nt(f_ref[span, :].astype(BF16), xb), d[span, :])
            part = dot_nn(rb, xb)
            if other:
                g_refs[0][pl.ds(c * block, block), :] = part
            else:
                g_refs[c][...] = part
        if halo:
            pack_halo(plan, xs, h_refs[:-1], h_refs[-1])
        if whole:
            x_out[...] = xs[pl.ds(PAD, minutes), :]

    if other:
        out_shape = [jax.ShapeDtypeStruct((plan.half, rank), F32)]
    else:
        out_shape = [jax.ShapeDtypeStruct((block, rank), F32) for _ in range(n_z)]
    n_g = len(out_shape)
    if halo:
        out_shape += halo_shapes(plan)
    if whole:
        out_shape.append(jax.ShapeDtypeStruct((minutes, rank), F32))
    outs = list(pl.pallas_call(
        kernel,
        in_specs=[VMEM] * (2 + n_x),
        out_specs=[VMEM] * len(out_shape),
        out_shape=out_shape,
        scratch_shapes=[pltpu.VMEM((minutes + 2 * PAD, rank), F32)],
        compiler_params=grant(16),
        name="load_other" if other else "load_mine",
    )(data, f, *xp))
    return outs[:n_g], outs[n_g:n_g + n_h], outs[n_g + n_h:]


def smoothing(plan, win, halos, lag_weights):
    rows, rank = plan.rows, plan.rank
    total = plan.minutes * plan.n_t

    def kernel(*refs):
        refs = list(refs)
        win_ref = refs.pop(0)
        h_refs = [refs.pop(0) for _ in plan.exchanges]
        w_ref, out, xw, far, near = refs
        s = lax.axis_index("series")
        t = lax.axis_index("tm")
        xw[...] = win_ref[...]

        def act(slot, part):
            kind, at, local, size, offset = part
            target, place = {"back": (near, at), "far": (far, at),
                             "prev": (xw, PAD - 1), "next": (xw, PAD + rows)}[kind]
            target[pl.ds(place, size), :] = h_refs[slot][pl.ds(offset, size), :]

        plan.each_part(False, act)
        w0 = w_ref[0:1, :]
        w1 = w_ref[1:2, :]
        x = xw[pl.ds(PAD, rows), :]
        here = t * plan.minutes + s * rows + lax.broadcasted_iota(jnp.int32, (rows, rank), 0)
        resid = x - w0 * xw[pl.ds(PAD - 1, rows), :] - w1 * near[pl.ds(0, rows), :]
        after_one = xw[pl.ds(PAD + 1, rows), :] - w0 * x - w1 * near[pl.ds(1, rows), :]
        after_far = far[pl.ds(1, rows), :] - w0 * far[pl.ds(0, rows), :] - w1 * x
        after_one = jnp.where(here + 1 < total, after_one, 0.0)
        after_far = jnp.where(here + LAG < total, after_far, 0.0)
        out[...] = smooth * (resid - w0 * after_one - w1 * after_far)

    return pl.pallas_call(
        kernel,
        in_specs=[VMEM] * (2 + len(plan.exchanges)),
        out_specs=VMEM,
        out_shape=jax.ShapeDtypeStruct((rows, rank), F32),
        scratch_shapes=[pltpu.VMEM((rows + 2 * PAD, rank), F32), pltpu.VMEM((up8(rows + 1), rank), F32),
                        pltpu.VMEM((up8(rows + 1), rank), F32)],
        compiler_params=grant(8),
        name="smoothing",
    )(win, *halos, lag_weights)


def assemble(plan, blocks):
    def kernel(*refs):
        for c, ref in enumerate(refs[:-1]):
            refs[-1][pl.ds(block_start(plan, c), plan.block), :] = ref[...]

    return pl.pallas_call(
        kernel,
        in_specs=[VMEM] * len(blocks),
        out_specs=VMEM,
        out_shape=jax.ShapeDtypeStruct((plan.series, plan.rank), F32),
        compiler_params=grant(8),
        name="assemble",
    )(*blocks)


def body(observed, mask, loadings, factors, lag_weights):
    n_s, n_t = lax.axis_size("series"), lax.axis_size("tm")
    plan = Plan(n_s, n_t, loadings.shape[0], factors.shape[0], loadings.shape[1])
    step_time = 1.0 / (plan.series * n_s / plan.rank + margin)
    step_load = 1.0 / (plan.minutes * n_t)
    rows, n_z, block = plan.rows, plan.n_z, plan.block

    def swap(value, axis, count, k):
        return lax.ppermute(value, axis, [(i, i ^ k) for i in range(count)])

    t = lax.axis_index("tm")
    own_start = (t % 2) * plan.half + (t // 2) * block
    own_loads = lax.dynamic_slice_in_dim(loadings, own_start, block, 0)
    loads = [loadings]
    data = [observed, mask]
    xp = [factors]
    halos = []
    for outer in range(OUTER):
        last = outer + 1 == OUTER
        for inner in range(TIME_STEPS):
            grads, made, extra = time_pass(plan, data, loads, xp, not halos)
            if len(data) > 1:
                data = [extra.pop()]
            if len(loads) > 1:
                loads = [extra.pop()]
            halos = halos or made
            got = [swap(grads[k], "series", n_s, k) for k in range(1, n_s)]
            sent = [lax.ppermute(h, "tm", pairs) for h, pairs in zip(halos[:-1], plan.pairs)]
            win = halos[-1]
            smooth_grad = smoothing(plan, win, sent, lag_weights)
            share = grads[0]
            for value in got:
                share = share + value
            own = win[PAD:PAD + rows] - step_time * (share + smooth_grad)
            xp = [own] + [swap(own, "series", n_s, k) for k in range(1, n_s)]
            halos = []
        (other,), _, _ = load_pass(plan, data[0], loads[0], xp, True, False, False)
        crossed = swap(other, "tm", n_t, 1)
        mine, halos, whole = load_pass(plan, data[0], loads[0], xp, False, not last, last)
        mine = [m + crossed[k * block:(k + 1) * block] for k, m in enumerate(mine)]
        total = mine[0]
        for k in range(1, n_z):
            total = total + swap(mine[k], "tm", n_t, 2 * k)
        own_loads = own_loads - step_load * (total + shrink * own_loads)
        near = [own_loads] + [swap(own_loads, "tm", n_t, 2 * k) for k in range(1, n_z)]
        loads = near + [swap(value, "tm", n_t, 1) for value in near]
    return (assemble(plan, loads), whole[0])


def solution(mesh):
    in_specs = (P("series", "tm"), P("series", "tm"), P("series", None), P("tm", None), P())
    out_specs = (P("series", None), P("tm", None))
    return jax.shard_map(body, mesh=mesh, in_specs=in_specs, out_specs=out_specs, check_vma=False)
```

```python
import jax
import jax.numpy as jnp
from jax import lax
from jax.experimental import pallas as pl
from jax.experimental.pallas import tpu as pltpu
from jax.sharding import PartitionSpec as P


LAG = 1440
OUTER = 2
TIME_STEPS = 2

smooth = 4.0
shrink = 0.1
margin = 32.0
hidden = 64.0
F32 = jnp.float32
BF16 = jnp.bfloat16
VMEM = pl.BlockSpec(memory_space=pltpu.VMEM)
ANY = pl.BlockSpec(memory_space=pl.ANY)


def dot_nt(a, b):
    return lax.dot_general(a, b, (((1,), (1,)), ((), ())), preferred_element_type=F32)


def dot_tn(a, b):
    return lax.dot_general(a, b, (((0,), (0,)), ((), ())), preferred_element_type=F32)


def dot_nn(a, b):
    return lax.dot_general(a, b, (((1,), (0,)), ((), ())), preferred_element_type=F32)


def up8(value):
    return -(-value // 8) * 8


class Plan:
    def __init__(self, n_s, n_t, series, minutes, rank):
        self.n_s, self.n_t, self.series, self.minutes, self.rank = n_s, n_t, series, minutes, rank
        self.rows = minutes // n_s
        self.n_z = n_t // 2
        self.block = series // n_t
        self.half = series // 2
        self.bits = self.n_z.bit_length() - 1
        assert 1 << self.bits == self.n_z
        span = 2 * minutes
        self.parts = []
        for s in range(n_s):
            per_core = []
            for core in range(2):
                first = core * minutes + s * self.rows
                wanted = [("near", first - LAG, self.rows + 1), ("far", first + LAG - 1, self.rows + 1),
                          ("prev", first - 1, 1), ("next", first + self.rows, 1)]
                listed = []
                for kind, row, count in wanted:
                    at = 0
                    while at < count:
                        step = (row + at) // span
                        local = (row + at) % span
                        size = min(count - at, span - local)
                        if step == 0 and local < minutes:
                            size = min(size, minutes - local)
                        listed.append((kind, at, step, local, size))
                        at += size
                assert all(abs(p[2]) <= 1 for p in listed)
                per_core.append(listed)
            self.parts.append(per_core)
        self.messages, longest = [], 8
        for s in range(n_s):
            by_step = {}
            for step in (-1, 1):
                offset, placed = 0, []
                for core in range(2):
                    for kind, at, found, local, size in self.parts[s][core]:
                        if found == step:
                            for low, high in ((0, minutes), (minutes, span)):
                                start, end = max(local, low), min(local + size, high)
                                if start < end:
                                    placed.append((core, kind, at + start - local, start, end - start, offset))
                                    offset += up8(end - start)
                by_step[step] = placed
                longest = max(longest, offset)
            self.messages.append(by_step)
        self.length = longest
        self.pairs = [(t, t + 2 * self.facing(t % 2, t // 2)) for t in range(n_t)
                      if 0 <= t + 2 * self.facing(t % 2, t // 2) < n_t]

    def facing(self, core, z):
        return 1 if (core + z) % 2 == 0 else -1


def chip_rows(plan, own, partner, core, local, size):
    half = local // plan.minutes
    ref = own if half == core else partner
    start = local - half * plan.minutes
    return ref[pl.ds(start, size), :]


def each_place(plan, act):
    s = lax.axis_index("series")
    t = lax.axis_index("tm")
    for value in range(plan.n_s):
        for core in range(2):
            for z in range(2):
                @pl.when(jnp.logical_and(s == value, t % 4 == 2 * z + core))
                def _():
                    act(value, core, plan.facing(core, z))


def call(kernel, ins, out_shape, scratch=(), mib=8):
    single = not isinstance(out_shape, list)
    outs = pl.pallas_call(
        kernel,
        in_specs=[VMEM] * len(ins),
        out_specs=VMEM if single else [VMEM] * len(out_shape),
        out_shape=out_shape,
        scratch_shapes=list(scratch),
        compiler_params=pltpu.CompilerParams(vmem_limit_bytes=mib * 2**20),
    )(*ins)
    return outs if single else list(outs)


def array(rows, rank):
    return jax.ShapeDtypeStruct((rows, rank), F32)


def gather(plan, pieces):
    def kernel(*refs):
        s = lax.axis_index("series")
        for k, ref in enumerate(refs[:-1]):
            start = pl.multiple_of(jnp.bitwise_xor(s, k) * plan.rows, plan.rows)
            refs[-1][pl.ds(start, plan.rows), :] = ref[...]

    return call(kernel, pieces, array(plan.minutes, plan.rank))


def pack(plan, x, partner, ahead):
    def kernel(own_ref, partner_ref, ahead_ref, out):
        def act(s, core, facing):
            for _, kind, at, local, size, offset in plan.messages[s][-facing]:
                out[pl.ds(offset, size), :] = chip_rows(plan, own_ref, partner_ref, core, local, size)

        each_place(plan, act)

    return call(kernel, [x, partner, ahead], array(plan.length, plan.rank))


def smoothing(plan, x, partner, got, shared, lag_weights):
    rows, rank = plan.rows, plan.rank
    total = plan.minutes * plan.n_t

    def kernel(x_ref, partner_ref, got_ref, shared_ref, w_ref, out, own_out, near, far, prev, after):
        s = lax.axis_index("series")
        t = lax.axis_index("tm")
        targets = {"near": near, "far": far, "prev": prev, "next": after}

        def act(value, core, facing):
            for kind, at, step, local, size in plan.parts[value][core]:
                if step == 0:
                    targets[kind][pl.ds(at, size), :] = chip_rows(plan, x_ref, partner_ref, core, local, size)
            for step in (-1, 1):
                ref = got_ref if step == facing else shared_ref
                for for_core, kind, at, local, size, offset in plan.messages[value][step]:
                    if for_core == core:
                        targets[kind][pl.ds(at, size), :] = ref[pl.ds(offset, size), :]

        each_place(plan, act)
        x = x_ref[pl.ds(pl.multiple_of(s * rows, rows), rows), :]
        own_out[...] = x
        place = lax.broadcasted_iota(jnp.int32, (rows, rank), 0)
        back_one = jnp.where(place == 0, prev[0:1, :], pltpu.roll(x, 1, 0))
        ahead_one = jnp.where(place == rows - 1, after[0:1, :], pltpu.roll(x, rows - 1, 0))
        w0 = w_ref[0:1, :]
        w1 = w_ref[1:2, :]
        here = t * plan.minutes + s * rows + place
        resid = x - w0 * back_one - w1 * near[pl.ds(0, rows), :]
        after_one = ahead_one - w0 * x - w1 * near[pl.ds(1, rows), :]
        after_far = far[pl.ds(1, rows), :] - w0 * far[pl.ds(0, rows), :] - w1 * x
        after_one = jnp.where(here + 1 < total, after_one, 0.0)
        after_far = jnp.where(here + LAG < total, after_far, 0.0)
        out[...] = smooth * (resid - w0 * after_one - w1 * after_far)

    tall = pltpu.VMEM((up8(rows + 1), rank), F32)
    one = pltpu.VMEM((8, rank), F32)
    return call(kernel, [x, partner, got, shared, lag_weights], [array(rows, rank)] * 2,
                [tall, tall, one, one])


def residual(prod, obs):
    obs = obs.astype(F32)
    return jnp.where(obs < 0.5 * hidden, prod - obs, 0.0).astype(BF16)


def order(plan, q):
    mirrored = sum(((q >> i) & 1) << (plan.bits - 1 - i) for i in range(plan.bits))
    return mirrored, q


def block_start(plan, other, q):
    t = lax.axis_index("tm")
    side = 1 - t % 2 if other else t % 2
    low, high = order(plan, q)
    z = jnp.bitwise_xor(t // 2, jnp.where(side == 0, low, high))
    return pl.multiple_of(side * plan.half + z * plan.block, plan.block)


def store_blocks(plan, places, refs, out):
    for (other, q, count), ref in zip(places, refs):
        for i in range(count):
            out[pl.ds(block_start(plan, other, q + i), plan.block), :] = (
                ref[pl.ds(i * plan.block, plan.block), :].astype(out.dtype))


def time_pass(plan, data, loads, places, x):
    first = len(data) == 2
    n_s, rows, series, minutes, rank = plan.n_s, plan.rows, plan.series, plan.minutes, plan.rank
    chunk = series // 4
    count = series // chunk
    n_f = len(loads)

    def kernel(*refs):
        refs = list(refs)
        d_refs = [refs.pop(0) for _ in data]
        f_refs = [refs.pop(0) for _ in loads]
        x_ref = refs.pop(0)
        g_refs = [refs.pop(0) for _ in range(n_s)]
        f = refs.pop(0) if n_f > 1 else f_refs[0]
        held = refs.pop(0) if first else d_refs[0]
        acc = refs.pop(0)
        if first:
            seen, sem = refs
            copies = []
            for c in range(count):
                span = pl.ds(c * chunk, chunk)
                copies.append([pltpu.make_async_copy(src.at[span, :], dst.at[span, :], sem.at[i, c])
                               for i, (src, dst) in enumerate(zip(d_refs, (held, seen)))])
            for group in copies:
                for copy in group:
                    copy.start()
        if n_f > 1:
            store_blocks(plan, places, f_refs, f)
        xb = x_ref[...].astype(BF16)
        for c in range(count):
            span = pl.ds(c * chunk, chunk)
            if first:
                for copy in copies[c]:
                    copy.wait()
                held[span, :] = jnp.where(seen[span, :] > 0, held[span, :], jnp.full((), hidden, BF16))
            fb = f[span, :].astype(BF16)
            part = dot_tn(fb, residual(dot_nt(fb, xb), held[span, :]))
            if c == 0:
                acc[...] = part
            else:
                acc[...] += part
        s = lax.axis_index("series")
        for k in range(n_s):
            start = pl.multiple_of(jnp.bitwise_xor(s, k) * rows, 128)
            g_refs[k][...] = acc[:, pl.ds(start, rows)].T

    out_shape = [array(rows, rank)] * n_s
    if n_f > 1:
        out_shape.append(jax.ShapeDtypeStruct((series, rank), BF16))
    if first:
        out_shape.append(jax.ShapeDtypeStruct((series, minutes), BF16))
    scratch = [pltpu.VMEM((rank, minutes), F32)]
    if first:
        scratch += [pltpu.VMEM((series, minutes), BF16), pltpu.SemaphoreType.DMA((2, count))]
    outs = list(pl.pallas_call(
        kernel,
        in_specs=[ANY if first else VMEM] * len(data) + [VMEM] * (n_f + 1),
        out_specs=[VMEM] * len(out_shape),
        out_shape=out_shape,
        scratch_shapes=scratch,
        compiler_params=pltpu.CompilerParams(vmem_limit_bytes=(24 if first else 16) * 2**20),
        name="time_pass",
    )(*data, *loads, x))
    return outs[:n_s], outs[n_s:]


def load_pass(plan, data, f, x, groups):
    block = plan.block

    def kernel(d, f_ref, x_ref, *g_refs):
        xb = x_ref[...].astype(BF16)
        for ref, (other, q, count) in zip(g_refs, groups):
            for i in range(count):
                span = pl.ds(block_start(plan, other, q + i), block)
                rb = residual(dot_nt(f_ref[span, :].astype(BF16), xb), d[span, :])
                ref[pl.ds(i * block, block), :] = dot_nn(rb, xb)

    return call(kernel, [data, f, x],
                [array(count * block, plan.rank) for other, q, count in groups], mib=16)


def update_loads(plan, own, parts, step):
    whole = own.shape[0] > plan.block

    def kernel(*refs):
        own_ref, p_refs, out = refs[0], refs[1:-1], refs[-1]
        total = p_refs[0][...]
        for ref in p_refs[1:]:
            total = total + ref[...]
        old = own_ref[pl.ds(block_start(plan, False, 0), plan.block), :] if whole else own_ref[...]
        out[...] = old - step * (total + shrink * old)

    return call(kernel, [own] + parts, array(plan.block, plan.rank))


def assemble(plan, blocks, places):
    def kernel(*refs):
        store_blocks(plan, places, refs[:-1], refs[-1])

    return call(kernel, blocks, array(plan.series, plan.rank))


def body(observed, mask, loadings, factors, lag_weights):
    n_s, n_t = lax.axis_size("series"), lax.axis_size("tm")
    plan = Plan(n_s, n_t, loadings.shape[0], factors.shape[0], loadings.shape[1])
    step_time = 1.0 / (plan.series * n_s / plan.rank + margin)
    step_load = 1.0 / (plan.minutes * n_t)
    n_z, block, bits = plan.n_z, plan.block, plan.bits

    def swap(value, axis, count, k):
        return lax.ppermute(value, axis, [(i, i ^ k) for i in range(count)])

    def swap_z(value, stage):
        bit = [stage, bits - 1 - stage]
        return lax.ppermute(value, "tm", [(i, i ^ (2 << bit[i % 2])) for i in range(n_t)])

    def smooth_all(x, partner, ahead):
        got = lax.ppermute(pack(plan, x, partner, ahead), "tm", plan.pairs)
        shared = swap(got, "tm", n_t, 1)
        return smoothing(plan, x, partner, got, shared, lag_weights)

    loads, places = [loadings], []
    data = [pltpu.with_memory_space_constraint(a, pltpu.HBM) for a in (observed, mask)]
    own_loads = loadings
    x = factors
    known = None
    for outer in range(OUTER):
        for _ in range(TIME_STEPS):
            partner = swap(x, "tm", n_t, 1) if known is None else None
            grads, extra = time_pass(plan, data, loads, places, x)
            if len(data) > 1:
                data = [extra.pop()]
            if len(loads) > 1:
                loads = [extra.pop()]
            smooth_grad, own = known or smooth_all(x, partner, grads[0])
            known = None
            got = [swap(grads[k], "series", n_s, k) for k in range(1, n_s)]
            share = grads[0]
            for value in got:
                share = share + value
            own = own - step_time * (share + smooth_grad)
            x = gather(plan, [own] + [swap(own, "series", n_s, k) for k in range(1, n_s)])
        top = n_z // 2
        other_high, = load_pass(plan, data[0], loads[0], x, [(True, top, top)])
        crossed_high = swap(other_high, "tm", n_t, 1)
        mine_high, = load_pass(plan, data[0], loads[0], x, [(False, top, top)])
        folded = swap_z(mine_high + crossed_high, 0)
        other_low, mine_low = load_pass(plan, data[0], loads[0], x, [(True, 0, top), (False, 0, top)])
        crossed_low = swap(other_low, "tm", n_t, 1)
        if outer + 1 < OUTER:
            known = smooth_all(x, swap(x, "tm", n_t, 1), mine_low)
        parts = [mine_low, crossed_low, folded]
        for stage in range(1, bits):
            size = n_z >> (stage + 1)
            send = sum(p[size * block:2 * size * block] for p in parts)
            parts = [p[:size * block] for p in parts] + [swap_z(send, stage)]
        own_loads = update_loads(plan, own_loads, parts, step_load)
        loads, places = [own_loads], [(False, 0, 1)]
        for stage in reversed(range(bits)):
            size = n_z >> (stage + 1)
            loads.append(swap_z(jnp.concatenate(loads, 0) if len(loads) > 1 else loads[0], stage))
            places.append((False, size, size))
        loads = loads + [swap(value, "tm", n_t, 1) for value in loads]
        places = places + [(True, q, count) for other, q, count in places]
    return (assemble(plan, loads, places), x)


def solution(mesh):
    in_specs = (P("series", "tm"), P("series", "tm"), P("series", None), P("tm", None), P())
    out_specs = (P("series", None), P("tm", None))
    return jax.shard_map(body, mesh=mesh, in_specs=in_specs, out_specs=out_specs, check_vma=False)
```
